32 devices in a mesh: gx: 8 (over z, y), gy: 4 (over x, core).
Axes of the slice: x: 2, y: 2, z: 4, core: 2. Of those that a mesh axis runs over, the one named last changes fastest.
Arguments:
- mass_per_volume: float32 [16, 256, 512], P(None, 'gx', 'gy'), may hold values from 0.5 to 2
- momentum: float32 [3, 16, 256, 512], P(None, None, 'gx', 'gy'), may hold values from -1 to 1
- energy: float32 [16, 256, 512], P(None, 'gx', 'gy'), may hold values from 4 to 6
Outputs:
- updated_state: float32 [5, 16, 256, 512], P(None, None, 'gx', 'gy')
The draws below stay inside these ranges and needn't reach their ends.
All inputs are finite; a program needn't handle non-finite values.
Results may differ from the reference program's by a relative error of at most 0.00012.
Values sent between devices are 32-bit elements; how exact they have to be, the bound alone decides.
A program may use at most 64 MiB of HBM per device.

```python
import math
import jax
import jax.numpy as jnp
from jax import lax

CX = 32
CY = 128
NZ = 16
NX = 256
NY = 512


def level_of(stream_key, shape, cuts, low, top_value):
    loudness = 1.0
    for dim, blocks in cuts:
        steps = jax.random.uniform(jax.random.fold_in(jax.random.fold_in(stream_key, 6), dim), (blocks,), jnp.float32, low / len(cuts), top_value / len(cuts))
        loudness = loudness * jnp.repeat(jnp.exp(steps), shape[dim] // blocks).reshape((-1,) + (1,) * (len(shape) - 1 - dim))
    return loudness


def gaussian(key, shape, scale, most, shards=(), kind=jnp.bfloat16):
    level = level_of(key, shape, shards, -0.22, 0.18) if shards else 1.0
    result = jax.random.normal(key, shape, jnp.float32) * scale * level
    return jnp.minimum(jnp.maximum(result, -most), most).astype(kind)


def setup_inputs(seed: int = 0) -> dict:
    arg_keys = jax.random.split(jax.random.key(seed), 4)
    mass_per_volume = jnp.clip(jnp.exp(math.log(2.0) - 1.3862944 * jax.random.uniform(arg_keys[0], (NZ, NX, NY), jnp.float32) ** level_of(arg_keys[0], (NZ, NX, NY), ((1, 8), (2, 4)), -0.2, 0.2)), 0.5, 2.0)
    momentum = gaussian(arg_keys[1], (3, NZ, NX, NY), 0.2, 1.0, ((2, 8), (3, 4)), jnp.float32)
    energy = jnp.clip(4.0 + 2.0 * jax.random.uniform(arg_keys[2], (NZ, NX, NY), jnp.float32) ** level_of(arg_keys[2], (NZ, NX, NY), ((1, 8), (2, 4)), -0.2, 0.2), 4.0, 6.0)
    return {"mass_per_volume": mass_per_volume, "momentum": momentum, "energy": energy}


gamma_ratio = 1.4
viscosity = 0.1
conductivity = 0.1 * 1.4 / (0.4 * 0.72)

def central(field, dimension):
    length = field.shape[dimension]
    widths = [(0, 0)] * field.ndim
    widths[dimension] = (3, 3)
    padded = jnp.pad(field, widths)

    def shifted_field(k):
        return lax.slice_in_dim(padded, 3 + k, 3 + k + length, axis=dimension)
    return 0.75 * (shifted_field(1) - shifted_field(-1)) - 0.15 * (shifted_field(2) - shifted_field(-2)) + 1.0 / 60.0 * (shifted_field(3) - shifted_field(-3))

def implicit_line(field, dimension, coefficient):
    extent = field.shape[dimension]
    position = jnp.arange(extent, dtype=jnp.int32)
    lower_band = jnp.where(position == 0, jnp.float32(0.0), jnp.float32(-coefficient))
    upper_band = jnp.where(position == extent - 1, jnp.float32(0.0), jnp.float32(coefficient))
    diagonal = jnp.ones((extent,), jnp.float32)
    results = []
    for member in range(field.shape[0]):
        moved = jnp.moveaxis(field[member], dimension - 1, 0)
        block_shape = moved.shape
        solved = lax.linalg.tridiagonal_solve(lower_band, diagonal, upper_band, moved.reshape(extent, -1))
        results.append(jnp.moveaxis(solved.reshape(block_shape), 0, dimension - 1))
    return jnp.stack(results, 0)

def derive_third(field):

    def rolled(k):
        return jnp.roll(field, -k, axis=1)
    return 0.75 * (rolled(1) - rolled(-1)) - 0.15 * (rolled(2) - rolled(-2)) + 1.0 / 60.0 * (rolled(3) - rolled(-3))

def flux_terms(mass_per_volume, momentum, energy, bulk_speed_vector, normal_thermodynamic_load, grads):
    dilation = grads[0][0] + grads[1][1] + grads[2][2]
    flux_vectors = []
    for j in range(3):
        entries = [momentum[j]]
        viscous_shear_power = jnp.zeros_like(mass_per_volume)
        for i in range(3):
            stress = viscosity * (grads[j][i] + grads[i][j])
            if i == j:
                stress = stress - 2.0 / 3.0 * viscosity * dilation
            momentum_flux = momentum[i] * bulk_speed_vector[j] - stress
            if i == j:
                momentum_flux = momentum_flux + normal_thermodynamic_load
            entries.append(momentum_flux)
            viscous_shear_power = viscous_shear_power + bulk_speed_vector[i] * stress
        entries.append((energy + normal_thermodynamic_load) * bulk_speed_vector[j] - viscous_shear_power - conductivity * grads[j][3])
        flux_vectors.append(jnp.stack(entries, 0))
    return flux_vectors

def reference(mass_per_volume, momentum, energy):
    coefficient = float(max(CX, CY))
    bulk_speed_vector = momentum / mass_per_volume[None]
    normal_thermodynamic_load = (gamma_ratio - 1.0) * (energy - 0.5 * jnp.sum(momentum * bulk_speed_vector, axis=0))
    thermal_level = normal_thermodynamic_load / mass_per_volume
    basic_physical_quantities = jnp.concatenate([bulk_speed_vector, thermal_level[None]], 0)
    grads = (central(basic_physical_quantities, 2), central(basic_physical_quantities, 3), derive_third(basic_physical_quantities))
    flux_vectors = flux_terms(mass_per_volume, momentum, energy, bulk_speed_vector, normal_thermodynamic_load, grads)
    divergence = central(flux_vectors[0], 2) + central(flux_vectors[1], 3) + derive_third(flux_vectors[2])
    source = -2.0 * coefficient * divergence
    partial_derivative_value = implicit_line(source, 2, coefficient)
    increment = implicit_line(partial_derivative_value, 3, coefficient)
    state = jnp.concatenate([mass_per_volume[None], momentum, energy[None]], 0)
    return state + increment
```

```python
import functools
import jax
import jax.numpy as jnp
import numpy as np
from jax import lax
from jax.experimental import pallas as pl
from jax.experimental.pallas import tpu as pltpu
from jax.sharding import PartitionSpec as P

viscosity = 0.1
conductivity = 0.1 * 1.4 / (0.4 * 0.72)
MESH = pl.DeviceIdType.MESH
WEIGHTS = {1: 0.75, -1: -0.75, 2: -0.15, -2: 0.15, 3: 1.0 / 60.0, -3: -1.0 / 60.0}
GROUPS = ((0, 2), (2, 5))


def local_inverse(length, coefficient):
    matrix = np.eye(length)
    matrix += coefficient * (np.eye(length, k=1) - np.eye(length, k=-1))
    return np.linalg.inv(matrix)


def reduced_tables(length, count, coefficient):
    inverse = local_inverse(length, coefficient)
    alpha, beta = coefficient * inverse[:, 0], -coefficient * inverse[:, -1]
    system = np.eye(2 * count)
    for b in range(count):
        for row, at in ((2 * b, 0), (2 * b + 1, length - 1)):
            if b > 0:
                system[row, 2 * b - 1] -= alpha[at]
            if b < count - 1:
                system[row, 2 * b + 2] -= beta[at]
    g = np.linalg.inv(system)
    up = [g[2 * b + 1, 2 * b : 2 * b + 2] for b in range(count)]
    down = [g[2 * b, 2 * b : 2 * b + 2] for b in range(count)]
    rows = []
    for b in range(count):
        prev = g[2 * b - 1] if b > 0 else np.zeros(2 * count)
        nxt = g[2 * b + 2] if b < count - 1 else np.zeros(2 * count)
        t = []
        for line in (prev, nxt):
            for d in range(1, count):
                other = (b - d) % count
                basis = up[other] if other < b else down[other]
                part = line[2 * other : 2 * other + 2]
                t.append(part @ basis / (basis @ basis))
        own = [*prev[2 * b : 2 * b + 2], *nxt[2 * b : 2 * b + 2]]
        rows.append([*up[b], *down[b], *own, *t])
    return np.asarray(rows).astype(np.float32), alpha, beta


def pivots(length, coefficient):
    inverse_pivot = np.ones(length)
    for i in range(1, length):
        inverse_pivot[i] = 1.0 / (1.0 + coefficient * coefficient * inverse_pivot[i - 1])
    return inverse_pivot


def lane_tables(ly, coefficient, alpha, beta):
    inverse = local_inverse(ly, coefficient)
    dy = np.zeros((ly, ly))
    for j in range(ly):
        for k, w in WEIGHTS.items():
            if 0 <= j + k < ly:
                dy[j + k, j] = w
    sel = np.zeros((5, 32, ly))
    ed = np.zeros((5, 32, ly))
    wy = np.zeros((5, 16, ly))
    ey = np.zeros((5, 16, ly))
    for f in range(5):
        for k in range(3):
            sel[f, 3 * f + k, k] = 1.0
            sel[f, 16 + 3 * f + k, ly - 3 + k] = 1.0
            for row, position in ((3 * f + k, k - 3), (16 + 3 * f + k, ly + k)):
                for step, w in WEIGHTS.items():
                    if 0 <= position - step < ly:
                        ed[f, row, position - step] = w
        wy[f, f], wy[f, 8 + f] = inverse[0], inverse[-1]
        ey[f, f], ey[f, 8 + f] = alpha, beta
    parts = [dy, inverse.T, sel.reshape(-1, ly), ed.reshape(-1, ly), wy.reshape(-1, ly), ey.reshape(-1, ly)]
    return np.concatenate(parts, 0).astype(np.float32)


def dot(a, b, dims):
    return lax.dot_general(
        a, b, (dims, ((), ())), precision=lax.Precision.HIGHEST, preferred_element_type=jnp.float32
    )


NN, NT, TN = ((1,), (0,)), ((1,), (1,)), ((0,), (0,))


def difference(at):
    return 0.75 * (at(1) - at(-1)) - 0.15 * (at(2) - at(-2)) + (1.0 / 60.0) * (at(3) - at(-3))


def around(v):
    n = v.shape[0]
    return difference(lambda k: pltpu.roll(v, (-k) % n, 0))


def kernel(
    nx, ny, lx, lz, ly, coefficient, ipiv, alpha, beta,
    mass, mom, energy, tab, xt, yt, out,
    xp, pt, ept, mt, gy, fxp, fy, dz, inc, ysend, yhalo, ysend2, yhalo2,
    xs, xr, ws, wr,
    hss, hrs, xss, xrs, wss, wrs,
):
    ix, iy = lax.axis_index("gx"), lax.axis_index("gy")
    rows = lx * lz

    barrier = pltpu.get_barrier_semaphore()
    for d in range(1, nx):
        pl.semaphore_signal(barrier, inc=1, device_id={"gx": lax.rem(ix + d, nx)}, device_id_type=MESH)
    for d in range(1, ny):
        pl.semaphore_signal(barrier, inc=1, device_id={"gy": lax.rem(iy + d, ny)}, device_id_type=MESH)

    o = 2 * ly
    dy = tab.at[pl.ds(0, ly)]
    inverse = tab.at[pl.ds(ly, ly)]

    def sel(f):
        return tab[o + 32 * f : o + 32 * f + 32]

    def ed(f):
        return tab[o + 160 + 32 * f : o + 160 + 32 * f + 32]

    def wy(f):
        return tab[o + 320 + 16 * f : o + 320 + 16 * f + 16]

    def ey(f):
        return tab[o + 400 + 16 * f : o + 400 + 16 * f + 16]

    def flat(v):
        return v.reshape(rows, ly)

    def primitives(i, _=None):
        at = pl.ds(i, lz, stride=lx)
        rho, e = mass[at, :], energy[at, :]
        m = [mom[k, at, :] for k in range(3)]
        inv = 1.0 / rho
        u = [a * inv for a in m]
        p = 0.4 * (e - 0.5 * (m[0] * u[0] + m[1] * u[1] + m[2] * u[2]))
        for k in range(3):
            xp[k, i + 3] = u[k]
            mt[k, i] = m[k]
        xp[3, i + 3] = p * inv
        pt[i] = p
        ept[i] = e + p
        return 0

    edges = sorted({*range(3), *range(lx - 3, lx)})
    for i in edges:
        primitives(i)

    zeros3 = jnp.zeros((3, lz, ly), jnp.float32)

    def x_halo(ref, fields, base):
        to_next = pltpu.make_async_remote_copy(
            ref.at[:, pl.ds(lx, 3)], ref.at[:, pl.ds(0, 3)], hss.at[base], hrs.at[base],
            device_id={"gx": ix + 1}, device_id_type=MESH)
        to_prev = pltpu.make_async_remote_copy(
            ref.at[:, pl.ds(3, 3)], ref.at[:, pl.ds(lx + 3, 3)], hss.at[base + 1], hrs.at[base + 1],
            device_id={"gx": ix - 1}, device_id_type=MESH)

        @pl.when(ix == 0)
        def _():
            for f in range(fields):
                ref[f, 0:3] = zeros3

        @pl.when(ix == nx - 1)
        def _():
            for f in range(fields):
                ref[f, lx + 3 : lx + 6] = zeros3

        return to_next, to_prev, ix, nx

    def y_halo(source, ref, base):
        to_next = pltpu.make_async_remote_copy(
            source.at[pl.ds(16, 16)], ref.at[pl.ds(0, 16)], hss.at[base], hrs.at[base],
            device_id={"gy": iy + 1}, device_id_type=MESH)
        to_prev = pltpu.make_async_remote_copy(
            source.at[pl.ds(0, 16)], ref.at[pl.ds(16, 16)], hss.at[base + 1], hrs.at[base + 1],
            device_id={"gy": iy - 1}, device_id_type=MESH)

        @pl.when(iy == 0)
        def _():
            ref[0:16] = jnp.zeros((16, rows), jnp.float32)

        @pl.when(iy == ny - 1)
        def _():
            ref[16:32] = jnp.zeros((16, rows), jnp.float32)

        return to_next, to_prev, iy, ny

    def start(halo):
        to_next, to_prev, here, count = halo
        pl.when(here < count - 1)(to_next.start)
        pl.when(here > 0)(to_prev.start)

    def arrive(halo):
        to_next, to_prev, here, count = halo
        pl.when(here > 0)(to_next.wait_recv)
        pl.when(here < count - 1)(to_prev.wait_recv)

    def sent(halo):
        to_next, to_prev, here, count = halo
        pl.when(here < count - 1)(to_next.wait_send)
        pl.when(here > 0)(to_prev.wait_send)

    h1x = x_halo(xp, 4, 0)
    pl.semaphore_wait(barrier, nx + ny - 2)
    start(h1x)
    lax.fori_loop(3, lx - 3, primitives, 0, unroll=2)

    packed = dot(sel(0), flat(xp[0, 3 : lx + 3]), NT)
    for f in range(1, 4):
        packed += dot(sel(f), flat(xp[f, 3 : lx + 3]), NT)
    ysend[...] = packed
    h1y = y_halo(ysend, yhalo, 2)
    start(h1y)
    for f in range(4):
        gy[f] = dot(flat(xp[f, 3 : lx + 3]), dy[...], NN).reshape(lx, lz, ly)
    arrive(h1y)
    for f in range(4):
        gy[f] += dot(yhalo[...], ed(f), TN).reshape(lx, lz, ly)
    arrive(h1x)

    def fluxes(i, _=None):
        u = [xp[k, i + 3] for k in range(3)]
        m = [mt[k, i] for k in range(3)]
        p, ep = pt[i], ept[i]
        g = [
            [difference(lambda k: xp[f, i + 3 + k]) for f in range(4)],
            [gy[f, i] for f in range(4)],
            [around(xp[f, i + 3]) for f in range(4)],
        ]
        dilation = (2.0 / 3.0 * viscosity) * (g[0][0] + g[1][1] + g[2][2])
        stress = {}
        for a in range(3):
            for b in range(a, 3):
                s = viscosity * (g[a][b] + g[b][a])
                if a == b:
                    s = s - dilation
                stress[a, b] = stress[b, a] = s
        for j in range(3):
            entries = [m[j]]
            for k in range(3):
                e = m[k] * u[j] - stress[k, j]
                entries.append(e + p if k == j else e)
            power = u[0] * stress[0, j] + u[1] * stress[1, j] + u[2] * stress[2, j]
            entries.append(ep * u[j] - power - conductivity * g[j][3])
            for c in range(5):
                if j == 0:
                    fxp[c, i + 3] = entries[c]
                elif j == 1:
                    fy[c, i] = entries[c]
                else:
                    dz[c, i] = around(entries[c])
        return 0

    for i in edges:
        fluxes(i)
    h2x = x_halo(fxp, 5, 4)
    start(h2x)
    lax.fori_loop(3, lx - 3, fluxes, 0)

    packed = dot(sel(0), flat(fy[0]), NT)
    for f in range(1, 5):
        packed += dot(sel(f), flat(fy[f]), NT)
    ysend2[...] = packed
    h2y = y_halo(ysend2, yhalo2, 6)
    start(h2y)
    for c in range(5):
        dz[c] += dot(flat(fy[c]), dy[...], NN).reshape(lx, lz, ly)
    arrive(h2y)
    for c in range(5):
        dz[c] += dot(yhalo2[...], ed(c), TN).reshape(lx, lz, ly)
    arrive(h2x)

    width = 8 + 2 * (nx - 1)

    def xtab(k):
        return xt[ix * width + k]

    copies = []
    ends = {}
    for g, (f0, f1) in enumerate(GROUPS):
        v = [None] * 5
        for i in range(lx):
            for f in range(f0, f1):
                s = difference(lambda k: fxp[f, i + 3 + k]) + dz[f, i]
                s = s * (-2.0 * coefficient)
                v[f] = s if i == 0 else (s + coefficient * v[f]) * float(ipiv[i])
                inc[f, i] = v[f]
        last = list(v)
        for i in range(lx - 2, -1, -1):
            for f in range(f0, f1):
                v[f] = inc[f, i] - float(coefficient * ipiv[i]) * v[f]
                inc[f, i] = v[f]
        for f in range(f0, f1):
            ends[f] = (v[f], last[f])
            xs[0, f] = xtab(0) * v[f] + xtab(1) * last[f]
            xs[1, f] = xtab(2) * v[f] + xtab(3) * last[f]
        for d in range(1, nx):
            which = jnp.where(ix + d >= nx, 1, 0).astype(jnp.int32)
            copy = pltpu.make_async_remote_copy(
                xs.at[which, pl.ds(f0, f1 - f0)], xr.at[d - 1, pl.ds(f0, f1 - f0)],
                xss.at[g, d - 1], xrs.at[g, d - 1],
                device_id={"gx": lax.rem(ix + d, nx)}, device_id_type=MESH)
            copy.start()
            copies.append((g, d, copy))

    edges_y = None
    for g, (f0, f1) in enumerate(GROUPS):
        for group, d, copy in copies:
            if group == g:
                copy.wait_recv()
        for f in range(f0, f1):
            y0, yl = inc[f, 0], inc[f, lx - 1]
            before = xtab(4) * y0 + xtab(5) * yl
            after = xtab(6) * y0 + xtab(7) * yl
            for d in range(1, nx):
                r = xr[d - 1, f]
                before += xtab(7 + d) * r
                after += xtab(7 + nx - 1 + d) * r
            for i in range(lx):
                inc[f, i] += float(alpha[i]) * before + float(beta[i]) * after
            part = dot(wy(f), flat(inc[f]), NT)
            edges_y = part if edges_y is None else edges_y + part

    ywidth = 8 + 2 * (ny - 1)

    def ytab(k):
        return yt[iy * ywidth + k]

    y0, yl = edges_y[0:8], edges_y[8:16]
    ws[0] = ytab(0) * y0 + ytab(1) * yl
    ws[1] = ytab(2) * y0 + ytab(3) * yl
    ycopies = []
    for d in range(1, ny):
        which = jnp.where(iy + d >= ny, 1, 0).astype(jnp.int32)
        copy = pltpu.make_async_remote_copy(
            ws.at[which], wr.at[d - 1], wss.at[d - 1], wrs.at[d - 1],
            device_id={"gy": lax.rem(iy + d, ny)}, device_id_type=MESH)
        copy.start()
        ycopies.append(copy)
    for f in range(5):
        gy5 = dot(flat(inc[f]), inverse[...], NN)
        inc[f] = gy5.reshape(lx, lz, ly)
    before = ytab(4) * y0 + ytab(5) * yl
    after = ytab(6) * y0 + ytab(7) * yl
    for d in range(1, ny):
        ycopies[d - 1].wait_recv()
        r = wr[d - 1]
        before += ytab(7 + d) * r
        after += ytab(7 + ny - 1 + d) * r
    outside = jnp.concatenate([before, after], 0)
    for f in range(5):
        total = (flat(inc[f]) + dot(outside, ey(f), TN)).reshape(lx, lz, ly)
        for i in range(lx):
            at = pl.ds(i, lz, stride=lx)
            state = mass[at, :] if f == 0 else (energy[at, :] if f == 4 else mt[f - 1, i])
            out[f, at, :] = state + total[i]

    for halo in (h1x, h1y, h2x, h2y):
        sent(halo)
    for _, _, copy in copies:
        copy.wait_send()
    for copy in ycopies:
        copy.wait_send()


def body(nx, ny, mass, mom, energy):
    lz, lx, ly = mass.shape
    rows = lx * lz
    coefficient = float(max(lx, ly))
    xtab, xa, xb = reduced_tables(lx, nx, coefficient)
    ytab, ya, yb = reduced_tables(ly, ny, coefficient)
    tab = lane_tables(ly, coefficient, ya, yb)
    vm = pl.BlockSpec(memory_space=pltpu.VMEM)
    sm = pl.BlockSpec(memory_space=pltpu.SMEM)
    f32 = jnp.float32
    groups = len(GROUPS)
    block = (lx, lz, ly)
    dma = pltpu.SemaphoreType.DMA
    result = pl.pallas_call(
        functools.partial(kernel, nx, ny, lx, lz, ly, coefficient, pivots(lx, coefficient), xa, xb),
        out_shape=jax.ShapeDtypeStruct((5, rows, ly), f32),
        in_specs=[vm, vm, vm, vm, sm, sm],
        out_specs=vm,
        scratch_shapes=[
            pltpu.VMEM((4, lx + 6, lz, ly), f32),
            pltpu.VMEM(block, f32),
            pltpu.VMEM(block, f32),
            pltpu.VMEM((3, *block), f32),
            pltpu.VMEM((4, *block), f32),
            pltpu.VMEM((5, lx + 6, lz, ly), f32),
            pltpu.VMEM((5, *block), f32),
            pltpu.VMEM((5, *block), f32),
            pltpu.VMEM((5, *block), f32),
            pltpu.VMEM((32, rows), f32),
            pltpu.VMEM((32, rows), f32),
            pltpu.VMEM((32, rows), f32),
            pltpu.VMEM((32, rows), f32),
            pltpu.VMEM((2, 5, lz, ly), f32),
            pltpu.VMEM((nx - 1, 5, lz, ly), f32),
            pltpu.VMEM((2, 8, rows), f32),
            pltpu.VMEM((ny - 1, 8, rows), f32),
            dma((8,)),
            dma((8,)),
            dma((groups, nx - 1)),
            dma((groups, nx - 1)),
            dma((ny - 1,)),
            dma((ny - 1,)),
        ],
        compiler_params=pltpu.CompilerParams(
            collective_id=0, has_side_effects=True, vmem_limit_bytes=48 * 2**20
        ),
    )(
        mass.reshape(rows, ly), mom.reshape(3, rows, ly), energy.reshape(rows, ly),
        jnp.asarray(tab), jnp.asarray(xtab.reshape(-1)), jnp.asarray(ytab.reshape(-1)),
    )
    return result.reshape(5, lz, lx, ly)


def solution(mesh):
    return jax.shard_map(
        functools.partial(body, mesh.shape["gx"], mesh.shape["gy"]),
        mesh=mesh,
        in_specs=(P(None, "gx", "gy"), P(None, None, "gx", "gy"), P(None, "gx", "gy")),
        out_specs=P(None, None, "gx", "gy"),
        check_vma=False,
    )
```

```python
import functools
import jax
import jax.numpy as jnp
import numpy as np
from jax import lax
from jax.experimental import pallas as pl
from jax.experimental.pallas import tpu as pltpu
from jax.sharding import PartitionSpec as P

viscosity = 0.1
conductivity = 0.1 * 1.4 / (0.4 * 0.72)
MESH = pl.DeviceIdType.MESH
WEIGHTS = {1: 45.0, -1: -45.0, 2: -9.0, -2: 9.0, 3: 1.0, -3: -1.0}
GROUPS = ((0, 2), (2, 4), (4, 5))


def local_inverse(length, coefficient):
    matrix = np.eye(length)
    matrix += coefficient * (np.eye(length, k=1) - np.eye(length, k=-1))
    return np.linalg.inv(matrix)


def reduced_tables(length, count, coefficient):
    inverse = local_inverse(length, coefficient)
    alpha, beta = coefficient * inverse[:, 0], -coefficient * inverse[:, -1]
    system = np.eye(2 * count)
    for b in range(count):
        for row, at in ((2 * b, 0), (2 * b + 1, length - 1)):
            if b > 0:
                system[row, 2 * b - 1] -= alpha[at]
            if b < count - 1:
                system[row, 2 * b + 2] -= beta[at]
    g = np.linalg.inv(system)
    up = [g[2 * b + 1, 2 * b : 2 * b + 2] for b in range(count)]
    down = [g[2 * b, 2 * b : 2 * b + 2] for b in range(count)]
    rows = []
    for b in range(count):
        prev = g[2 * b - 1] if b > 0 else np.zeros(2 * count)
        nxt = g[2 * b + 2] if b < count - 1 else np.zeros(2 * count)
        t = []
        for line in (prev, nxt):
            for d in range(1, count):
                other = (b - d) % count
                basis = up[other] if other < b else down[other]
                part = line[2 * other : 2 * other + 2]
                t.append(part @ basis / (basis @ basis))
        own = [*prev[2 * b : 2 * b + 2], *nxt[2 * b : 2 * b + 2]]
        rows.append([*up[b], *down[b], *own, *t])
    return np.asarray(rows).astype(np.float32), alpha, beta


def pivots(length, coefficient):
    inverse_pivot = np.ones(length)
    for i in range(1, length):
        inverse_pivot[i] = 1.0 / (1.0 + coefficient * coefficient * inverse_pivot[i - 1])
    return inverse_pivot


def halves(table):
    hi = table.astype(np.float32).astype(jnp.bfloat16)
    lo = (table - hi.astype(np.float64)).astype(np.float32).astype(jnp.bfloat16)
    return hi.astype(np.float32), lo.astype(np.float32)


def lane_tables(lx, lz, ly, coefficient, xa, xb, alpha, beta):
    inverse = local_inverse(ly, coefficient)
    dy = np.zeros((ly, ly))
    for j in range(ly):
        for k, w in WEIGHTS.items():
            if 0 <= j + k < ly:
                dy[j + k, j] = w
    sel = np.zeros((5, 32, ly))
    ed = np.zeros((32, 5 * ly))
    wy = np.zeros((5, 16, ly))
    ey = np.zeros((16, 5 * ly))
    for f in range(5):
        for k in range(3):
            sel[f, 3 * f + k, k] = 1.0
            sel[f, 16 + 3 * f + k, ly - 3 + k] = 1.0
            for row, position in ((3 * f + k, k - 3), (16 + 3 * f + k, ly + k)):
                for step, w in WEIGHTS.items():
                    if 0 <= position - step < ly:
                        ed[row, f * ly + position - step] = w
        wy[f, f], wy[f, 8 + f] = inverse[0], inverse[-1]
        ey[f, f * ly : (f + 1) * ly], ey[8 + f, f * ly : (f + 1) * ly] = alpha, beta
    ex = np.concatenate([np.kron(np.asarray(v)[None, :], np.eye(lz)) for v in (xa, xb)], 0)
    lhi, llo = halves(inverse.T)
    whi, wlo = halves(wy)
    ehi, elo = halves(ey)
    xhi, xlo = halves(ex)
    zero = np.zeros_like(lhi)
    tables = [
        np.concatenate([dy, dy], 0),
        np.block([[lhi, llo], [lhi, zero]]),
        np.concatenate([sel, sel], 2),
        np.concatenate([ed, ed], 0),
        np.concatenate([np.concatenate([whi, whi], 2), np.concatenate([wlo, 0 * wlo], 2)], 1),
        np.concatenate([ehi, ehi, elo], 0),
        np.concatenate([xhi, xhi, xlo], 0),
    ]
    return [t.astype(np.float32).astype(jnp.bfloat16) for t in tables]


def dot(a, b, dims):
    return lax.dot_general(a, b, (dims, ((), ())), preferred_element_type=jnp.float32)


def split(v):
    hi = v.astype(jnp.bfloat16)
    return hi, (v - hi.astype(jnp.float32)).astype(jnp.bfloat16)


NN, NT, TN = ((1,), (0,)), ((1,), (1,)), ((0,), (0,))


def difference(at):
    return 0.75 * (at(1) - at(-1)) - 0.15 * (at(2) - at(-2)) + (1.0 / 60.0) * (at(3) - at(-3))


def around(v):
    n = v.shape[0]
    return difference(lambda k: pltpu.roll(v, (-k) % n, 0))


def kernel(
    nx, ny, lx, lz, ly, coefficient, ipiv, xa, xb,
    mass_hbm, mom_hbm, energy_hbm, coef_hbm, *rest,
):
    tables_hbm, (out_hbm, mass, mom, energy, coef, *rest) = rest[:7], rest[7:]
    tables, rest = rest[:7], rest[7:]
    (
        iss, oss, out, xp, p2, pt, ept, mt, gy, fxp, f2, dz, inc, v2,
        ysend, yhalo, ysend2, yhalo2, xs, xr, ws, wr, hss, hrs, xss, xrs, wss, wrs,
    ) = rest
    dy_tab, inv_tab, sel_tab, ed_tab, wy_tab, ey_tab, ex_tab = tables
    ix, iy = lax.axis_index("gx"), lax.axis_index("gy")
    rows = lx * lz
    sources = (mass_hbm, energy_hbm, mom_hbm, coef_hbm, *tables_hbm)
    targets = (mass, energy, mom, coef, *tables)
    fetches = [
        pltpu.make_async_copy(a, b, iss.at[k]) for k, (a, b) in enumerate(zip(sources, targets))
    ]
    for fetch in fetches:
        fetch.start()

    barrier = pltpu.get_barrier_semaphore()
    for d in range(1, nx):
        pl.semaphore_signal(barrier, inc=1, device_id={"gx": lax.rem(ix + d, nx)}, device_id_type=MESH)
    for d in range(1, ny):
        pl.semaphore_signal(barrier, inc=1, device_id={"gy": lax.rem(iy + d, ny)}, device_id_type=MESH)

    def put(ref, at, v):
        hi, lo = split(v)
        ref[(*at, slice(None), slice(0, ly))] = hi
        ref[(*at, slice(None), slice(ly, 2 * ly))] = lo

    def wide(ref, f):
        return ref[f].reshape(rows, 2 * ly)

    def outer(f, v):
        return v[:, f * ly : (f + 1) * ly].reshape(lx, lz, ly)

    def flat(v):
        return v.reshape(rows, ly)

    def primitives(i, _=None):
        at = pl.ds(i, lz, stride=lx)
        rho, e = mass[at, :], energy[at, :]
        m = [mom[k, at, :] for k in range(3)]
        inv = 1.0 / rho
        u = [a * inv for a in m]
        p = 0.4 * (e - 0.5 * (m[0] * u[0] + m[1] * u[1] + m[2] * u[2]))
        for k in range(3):
            xp[k, i + 3] = u[k]
            mt[k, i] = m[k]
            put(p2, (k, i), u[k])
        xp[3, i + 3] = p * inv
        put(p2, (3, i), p * inv)
        pt[i] = p
        ept[i] = e + p
        return 0

    for fetch in fetches[:3]:
        fetch.wait()
    edges = sorted({*range(3), *range(lx - 3, lx)})
    for i in edges:
        primitives(i)

    zeros3 = jnp.zeros((3, lz, ly), jnp.float32)

    def x_halo(ref, fields, base):
        to_next = pltpu.make_async_remote_copy(
            ref.at[:, pl.ds(lx, 3)], ref.at[:, pl.ds(0, 3)], hss.at[base], hrs.at[base],
            device_id={"gx": ix + 1}, device_id_type=MESH)
        to_prev = pltpu.make_async_remote_copy(
            ref.at[:, pl.ds(3, 3)], ref.at[:, pl.ds(lx + 3, 3)], hss.at[base + 1], hrs.at[base + 1],
            device_id={"gx": ix - 1}, device_id_type=MESH)

        @pl.when(ix == 0)
        def _():
            for f in range(fields):
                ref[f, 0:3] = zeros3

        @pl.when(ix == nx - 1)
        def _():
            for f in range(fields):
                ref[f, lx + 3 : lx + 6] = zeros3

        return to_next, to_prev, ix, nx

    def y_halo(source, ref, base):
        to_next = pltpu.make_async_remote_copy(
            source.at[pl.ds(16, 16)], ref.at[pl.ds(0, 16)], hss.at[base], hrs.at[base],
            device_id={"gy": iy + 1}, device_id_type=MESH)
        to_prev = pltpu.make_async_remote_copy(
            source.at[pl.ds(0, 16)], ref.at[pl.ds(16, 16)], hss.at[base + 1], hrs.at[base + 1],
            device_id={"gy": iy - 1}, device_id_type=MESH)

        @pl.when(iy == 0)
        def _():
            ref[0:16] = jnp.zeros((16, rows), jnp.float32)

        @pl.when(iy == ny - 1)
        def _():
            ref[16:32] = jnp.zeros((16, rows), jnp.float32)

        return to_next, to_prev, iy, ny

    def start(halo):
        to_next, to_prev, here, count = halo
        pl.when(here < count - 1)(to_next.start)
        pl.when(here > 0)(to_prev.start)

    def arrive(halo):
        to_next, to_prev, here, count = halo
        pl.when(here > 0)(to_next.wait_recv)
        pl.when(here < count - 1)(to_prev.wait_recv)

    def sent(halo):
        to_next, to_prev, here, count = halo
        pl.when(here < count - 1)(to_next.wait_send)
        pl.when(here > 0)(to_prev.wait_send)

    h1x = x_halo(xp, 4, 0)
    pl.semaphore_wait(barrier, nx + ny - 2)
    start(h1x)
    lax.fori_loop(3, lx - 3, primitives, 0, unroll=2)

    for fetch in fetches[3:]:
        fetch.wait()
    packed = dot(sel_tab[0], wide(p2, 0), NT)
    for f in range(1, 4):
        packed += dot(sel_tab[f], wide(p2, f), NT)
    ysend[...] = packed
    h1y = y_halo(ysend, yhalo, 2)
    start(h1y)
    for f in range(4):
        gy[f] = dot(wide(p2, f), dy_tab[...], NN).reshape(lx, lz, ly)
    arrive(h1y)
    rim = dot(jnp.concatenate(split(yhalo[...]), 0), ed_tab[:, : 4 * ly], TN)
    for f in range(4):
        gy[f] = (gy[f] + outer(f, rim)) * (1.0 / 60.0)
    arrive(h1x)

    def fluxes(i, _=None):
        u = [xp[k, i + 3] for k in range(3)]
        m = [mt[k, i] for k in range(3)]
        p, ep = pt[i], ept[i]
        g = [
            [difference(lambda k: xp[f, i + 3 + k]) for f in range(4)],
            [gy[f, i] for f in range(4)],
            [around(xp[f, i + 3]) for f in range(4)],
        ]
        dilation = (2.0 / 3.0 * viscosity) * (g[0][0] + g[1][1] + g[2][2])
        stress = {}
        for a in range(3):
            for b in range(a, 3):
                s = viscosity * (g[a][b] + g[b][a])
                if a == b:
                    s = s - dilation
                stress[a, b] = stress[b, a] = s
        for j in range(3):
            entries = [m[j]]
            for k in range(3):
                e = m[k] * u[j] - stress[k, j]
                entries.append(e + p if k == j else e)
            power = u[0] * stress[0, j] + u[1] * stress[1, j] + u[2] * stress[2, j]
            entries.append(ep * u[j] - power - conductivity * g[j][3])
            for c in range(5):
                if j == 0:
                    fxp[c, i + 3] = entries[c]
                elif j == 1:
                    put(f2, (c, i), entries[c])
                else:
                    dz[c, i] = around(entries[c])
        return 0

    for i in edges:
        fluxes(i)
    h2x = x_halo(fxp, 5, 4)
    start(h2x)
    lax.fori_loop(3, lx - 3, fluxes, 0)

    packed = dot(sel_tab[0], wide(f2, 0), NT)
    for f in range(1, 5):
        packed += dot(sel_tab[f], wide(f2, f), NT)
    ysend2[...] = packed
    h2y = y_halo(ysend2, yhalo2, 6)
    start(h2y)
    for c in range(5):
        dz[c] += dot(wide(f2, c), dy_tab[...], NN).reshape(lx, lz, ly) * (1.0 / 60.0)
    arrive(h2y)
    rim = dot(jnp.concatenate(split(yhalo2[...]), 0), ed_tab[...], TN)
    for c in range(5):
        dz[c] += outer(c, rim) * (1.0 / 60.0)
    arrive(h2x)

    width = 8 + 2 * (nx - 1)

    def xtab(k):
        return coef[ix * width + k]

    copies = []
    ends = {}
    for g, (f0, f1) in enumerate(GROUPS):
        v = [None] * 5
        for i in range(lx):
            for f in range(f0, f1):
                s = difference(lambda k: fxp[f, i + 3 + k]) + dz[f, i]
                s = s * (-2.0 * coefficient)
                v[f] = s if i == 0 else (s + coefficient * v[f]) * float(ipiv[i])
                inc[f, i] = v[f]
        last = list(v)
        for f in range(f0, f1):
            put(v2, (f, lx - 1), v[f])
        for i in range(lx - 2, -1, -1):
            for f in range(f0, f1):
                v[f] = inc[f, i] - float(coefficient * ipiv[i]) * v[f]
                put(v2, (f, i), v[f])
        for f in range(f0, f1):
            ends[f] = (v[f], last[f])
            xs[0, f] = xtab(0) * v[f] + xtab(1) * last[f]
            xs[1, f] = xtab(2) * v[f] + xtab(3) * last[f]
        for d in range(1, nx):
            which = jnp.where(ix + d >= nx, 1, 0).astype(jnp.int32)
            copy = pltpu.make_async_remote_copy(
                xs.at[which, pl.ds(f0, f1 - f0)], xr.at[d - 1, pl.ds(f0, f1 - f0)],
                xss.at[g, d - 1], xrs.at[g, d - 1],
                device_id={"gx": lax.rem(ix + d, nx)}, device_id_type=MESH)
            copy.start()
            copies.append((g, d, copy))

    edges_y = dot(wy_tab[0], wide(v2, 0), NT)
    for f in range(1, 5):
        edges_y += dot(wy_tab[f], wide(v2, f), NT)
    for f in range(5):
        both = dot(wide(v2, f), inv_tab[...], NN)
        inc[f] = (both[:, :ly] + both[:, ly:]).reshape(lx, lz, ly)
    outside_x = []
    edges_x = None
    for g, (f0, f1) in enumerate(GROUPS):
        for group, d, copy in copies:
            if group == g:
                copy.wait_recv()
        for f in range(f0, f1):
            y0, yl = ends[f]
            before = xtab(4) * y0 + xtab(5) * yl
            after = xtab(6) * y0 + xtab(7) * yl
            for d in range(1, nx):
                r = xr[d - 1, f]
                before += xtab(7 + d) * r
                after += xtab(7 + nx - 1 + d) * r
            pair = jnp.concatenate(split(jnp.concatenate([before, after], 0)), 1)
            outside_x.append(pair)
            part = dot(wy_tab[f], pair, NT)
            edges_x = part if edges_x is None else edges_x + part
    edges_x = edges_x[:16] + edges_x[16:]
    hi, lo = split(edges_x)
    edges_y = edges_y[:16] + edges_y[16:] + dot(jnp.concatenate([hi, lo, hi], 1), ex_tab[...], NN)

    ywidth = 8 + 2 * (ny - 1)

    def ytab(k):
        return coef[nx * width + iy * ywidth + k]

    y0, yl = edges_y[0:8], edges_y[8:16]
    ws[0] = ytab(0) * y0 + ytab(1) * yl
    ws[1] = ytab(2) * y0 + ytab(3) * yl
    ycopies = []
    for d in range(1, ny):
        which = jnp.where(iy + d >= ny, 1, 0).astype(jnp.int32)
        copy = pltpu.make_async_remote_copy(
            ws.at[which], wr.at[d - 1], wss.at[d - 1], wrs.at[d - 1],
            device_id={"gy": lax.rem(iy + d, ny)}, device_id_type=MESH)
        copy.start()
        ycopies.append(copy)
    both = dot(jnp.concatenate(outside_x, 0), inv_tab[...], NN)
    across = (both[:, :ly] + both[:, ly:]).reshape(5, 2, lz, ly)
    before = ytab(4) * y0 + ytab(5) * yl
    after = ytab(6) * y0 + ytab(7) * yl
    for d in range(1, ny):
        ycopies[d - 1].wait_recv()
        r = wr[d - 1]
        before += ytab(7 + d) * r
        after += ytab(7 + ny - 1 + d) * r
    hi, lo = split(jnp.concatenate([before, after], 0))
    rim = dot(jnp.concatenate([hi, lo, hi], 0), ey_tab[...], TN)
    stores = []
    for f in range(5):
        total = outer(f, rim)
        for i in range(lx):
            at = pl.ds(i, lz, stride=lx)
            state = mass[at, :] if f == 0 else (energy[at, :] if f == 4 else mt[f - 1, i])
            step = float(xa[i]) * across[f, 0] + float(xb[i]) * across[f, 1]
            out[f, at, :] = (state + inc[f, i]) + (step + total[i])
        store = pltpu.make_async_copy(out.at[f], out_hbm.at[f], oss.at[f])
        store.start()
        stores.append(store)
    for store in stores:
        store.wait()

    for halo in (h1x, h1y, h2x, h2y):
        sent(halo)
    for _, _, copy in copies:
        copy.wait_send()
    for copy in ycopies:
        copy.wait_send()


def body(nx, ny, mass, mom, energy):
    lz, lx, ly = mass.shape
    rows = lx * lz
    coefficient = float(max(lx, ly))
    xtab, xa, xb = reduced_tables(lx, nx, coefficient)
    ytab, ya, yb = reduced_tables(ly, ny, coefficient)
    tables = lane_tables(lx, lz, ly, coefficient, xa, xb, ya, yb)
    coef = np.concatenate([xtab.reshape(-1), ytab.reshape(-1)])
    coef = np.pad(coef, (0, -coef.size % 1024))
    f32 = jnp.float32
    groups = len(GROUPS)
    block = (lx, lz, ly)
    dma = pltpu.SemaphoreType.DMA
    result = pl.pallas_call(
        functools.partial(kernel, nx, ny, lx, lz, ly, coefficient, pivots(lx, coefficient), xa, xb),
        out_shape=jax.ShapeDtypeStruct((5, rows, ly), f32),
        in_specs=[pl.BlockSpec(memory_space=pltpu.HBM)] * 11,
        out_specs=pl.BlockSpec(memory_space=pltpu.HBM),
        scratch_shapes=[
            pltpu.VMEM((rows, ly), f32),
            pltpu.VMEM((3, rows, ly), f32),
            pltpu.VMEM((rows, ly), f32),
            pltpu.SMEM(coef.shape, f32),
            *[pltpu.VMEM(t.shape, t.dtype) for t in tables],
            dma((11,)),
            dma((5,)),
            pltpu.VMEM((5, rows, ly), f32),
            pltpu.VMEM((4, lx + 6, lz, ly), f32),
            pltpu.VMEM((4, lx, lz, 2 * ly), jnp.bfloat16),
            pltpu.VMEM(block, f32),
            pltpu.VMEM(block, f32),
            pltpu.VMEM((3, *block), f32),
            pltpu.VMEM((4, *block), f32),
            pltpu.VMEM((5, lx + 6, lz, ly), f32),
            pltpu.VMEM((5, lx, lz, 2 * ly), jnp.bfloat16),
            pltpu.VMEM((5, *block), f32),
            pltpu.VMEM((5, *block), f32),
            pltpu.VMEM((5, lx, lz, 2 * ly), jnp.bfloat16),
            pltpu.VMEM((32, rows), f32),
            pltpu.VMEM((32, rows), f32),
            pltpu.VMEM((32, rows), f32),
            pltpu.VMEM((32, rows), f32),
            pltpu.VMEM((2, 5, lz, ly), f32),
            pltpu.VMEM((nx - 1, 5, lz, ly), f32),
            pltpu.VMEM((2, 8, rows), f32),
            pltpu.VMEM((ny - 1, 8, rows), f32),
            dma((8,)),
            dma((8,)),
            dma((groups, nx - 1)),
            dma((groups, nx - 1)),
            dma((ny - 1,)),
            dma((ny - 1,)),
        ],
        compiler_params=pltpu.CompilerParams(
            collective_id=0, has_side_effects=True, vmem_limit_bytes=67043328
        ),
    )(
        mass.reshape(rows, ly), mom.reshape(3, rows, ly), energy.reshape(rows, ly),
        jnp.asarray(coef), *[jnp.asarray(t) for t in tables],
    )
    return result.reshape(5, lz, lx, ly)


def solution(mesh):
    return jax.shard_map(
        functools.partial(body, mesh.shape["gx"], mesh.shape["gy"]),
        mesh=mesh,
        in_specs=(P(None, "gx", "gy"), P(None, None, "gx", "gy"), P(None, "gx", "gy")),
        out_specs=P(None, None, "gx", "gy"),
        check_vma=False,
    )
```

```python
import functools
import jax
import jax.numpy as jnp
import numpy as np
from jax import lax
from jax.experimental import pallas as pl
from jax.experimental.pallas import tpu as pltpu
from jax.sharding import PartitionSpec as P

viscosity = 0.1
conductivity = 0.1 * 1.4 / (0.4 * 0.72)
MESH = pl.DeviceIdType.MESH
WEIGHTS = {1: 45.0, -1: -45.0, 2: -9.0, -2: 9.0, 3: 1.0, -3: -1.0}
GROUPS = ((0, 2), (2, 4), (4, 5))


def local_inverse(length, coefficient):
    matrix = np.eye(length)
    matrix += coefficient * (np.eye(length, k=1) - np.eye(length, k=-1))
    return np.linalg.inv(matrix)


def reduced_tables(length, count, coefficient):
    inverse = local_inverse(length, coefficient)
    alpha, beta = coefficient * inverse[:, 0], -coefficient * inverse[:, -1]
    system = np.eye(2 * count)
    for b in range(count):
        for row, at in ((2 * b, 0), (2 * b + 1, length - 1)):
            if b > 0:
                system[row, 2 * b - 1] -= alpha[at]
            if b < count - 1:
                system[row, 2 * b + 2] -= beta[at]
    g = np.linalg.inv(system)
    up = [g[2 * b + 1, 2 * b : 2 * b + 2] for b in range(count)]
    down = [g[2 * b, 2 * b : 2 * b + 2] for b in range(count)]
    rows = []
    for b in range(count):
        prev = g[2 * b - 1] if b > 0 else np.zeros(2 * count)
        nxt = g[2 * b + 2] if b < count - 1 else np.zeros(2 * count)
        t = []
        for line in (prev, nxt):
            for d in range(1, count):
                other = (b - d) % count
                basis = up[other] if other < b else down[other]
                part = line[2 * other : 2 * other + 2]
                t.append(part @ basis / (basis @ basis))
        own = [*prev[2 * b : 2 * b + 2], *nxt[2 * b : 2 * b + 2]]
        rows.append([*up[b], *down[b], *own, *t])
    return np.asarray(rows).astype(np.float32), alpha, beta


def pivots(length, coefficient):
    inverse_pivot = np.ones(length)
    for i in range(1, length):
        inverse_pivot[i] = 1.0 / (1.0 + coefficient * coefficient * inverse_pivot[i - 1])
    return inverse_pivot


def halves(table):
    hi = table.astype(np.float32).astype(jnp.bfloat16)
    lo = (table - hi.astype(np.float64)).astype(np.float32).astype(jnp.bfloat16)
    return hi.astype(np.float32), lo.astype(np.float32)


def lane_tables(lx, lz, ly, coefficient, xa, xb, alpha, beta):
    inverse = local_inverse(ly, coefficient)
    dy = np.zeros((ly, ly))
    for j in range(ly):
        for k, w in WEIGHTS.items():
            if 0 <= j + k < ly:
                dy[j + k, j] = w
    sel = np.zeros((5, 32, ly))
    ed = np.zeros((32, 5 * ly))
    wy = np.zeros((5, 16, ly))
    ey = np.zeros((16, 5 * ly))
    for f in range(5):
        for k in range(3):
            sel[f, 3 * f + k, k] = 1.0
            sel[f, 16 + 3 * f + k, ly - 3 + k] = 1.0
            for row, position in ((3 * f + k, k - 3), (16 + 3 * f + k, ly + k)):
                for step, w in WEIGHTS.items():
                    if 0 <= position - step < ly:
                        ed[row, f * ly + position - step] = w
        wy[f, f], wy[f, 8 + f] = inverse[0], inverse[-1]
        ey[f, f * ly : (f + 1) * ly], ey[8 + f, f * ly : (f + 1) * ly] = alpha, beta
    ex = np.concatenate([np.kron(np.asarray(v)[None, :], np.eye(lz)) for v in (xa, xb)], 0)
    lhi, llo = halves(inverse.T)
    whi, wlo = halves(wy)
    ehi, elo = halves(ey)
    xhi, xlo = halves(ex)
    zero = np.zeros_like(lhi)
    tables = [
        np.concatenate([dy, dy], 0),
        np.block([[lhi, llo], [lhi, zero]]),
        np.concatenate([sel, sel], 2),
        np.concatenate([ed, ed], 0),
        np.concatenate([np.concatenate([whi, whi], 2), np.concatenate([wlo, 0 * wlo], 2)], 1),
        np.concatenate([ehi, ehi, elo], 0),
        np.concatenate([xhi, xhi, xlo], 0),
    ]
    return [t.astype(np.float32).astype(jnp.bfloat16) for t in tables]


def dot(a, b, dims):
    return lax.dot_general(a, b, (dims, ((), ())), preferred_element_type=jnp.float32)


def split(v):
    hi = v.astype(jnp.bfloat16)
    return hi, (v - hi.astype(jnp.float32)).astype(jnp.bfloat16)


NN, NT, TN = ((1,), (0,)), ((1,), (1,)), ((0,), (0,))


def difference(at):
    return 0.75 * (at(1) - at(-1)) - 0.15 * (at(2) - at(-2)) + (1.0 / 60.0) * (at(3) - at(-3))


def around(v):
    n = v.shape[0]
    return difference(lambda k: pltpu.roll(v, (-k) % n, 0))


def kernel(
    nx, ny, lx, lz, ly, coefficient, ipiv, xa, xb,
    mass_hbm, mom_hbm, energy_hbm, coef_hbm, *rest,
):
    tables_hbm, (out_hbm, mass, energy, coef, *rest) = rest[:7], rest[7:]
    tables, rest = rest[:7], rest[7:]
    (
        iss, oss, out, xp, p2, pt, ept, mt, gy, fxp, f2, dz, inc, v2,
        ysend, yhalo, ysend2, yhalo2, xs, xr, ws, wr, hss, hrs, xss, xrs, wss, wrs,
    ) = rest
    dy_tab, inv_tab, sel_tab, ed_tab, wy_tab, ey_tab, ex_tab = tables
    ix, iy = lax.axis_index("gx"), lax.axis_index("gy")
    rows = lx * lz
    fetches = []
    for z in range(lz):
        fetches.append(pltpu.make_async_copy(mass_hbm.at[z], mass.at[:, z, :], iss.at[0]))
        fetches.append(pltpu.make_async_copy(energy_hbm.at[z], energy.at[:, z, :], iss.at[0]))
        for k in range(3):
            fetches.append(pltpu.make_async_copy(mom_hbm.at[k, z], mt.at[k, :, z, :], iss.at[0]))
    small = [
        pltpu.make_async_copy(a, b, iss.at[1 + k])
        for k, (a, b) in enumerate(zip((coef_hbm, *tables_hbm), (coef, *tables)))
    ]
    for fetch in (*fetches, *small):
        fetch.start()

    barrier = pltpu.get_barrier_semaphore()
    for d in range(1, nx):
        pl.semaphore_signal(barrier, inc=1, device_id={"gx": lax.rem(ix + d, nx)}, device_id_type=MESH)
    for d in range(1, ny):
        pl.semaphore_signal(barrier, inc=1, device_id={"gy": lax.rem(iy + d, ny)}, device_id_type=MESH)

    def put(ref, at, v):
        hi, lo = split(v)
        ref[(*at, slice(None), slice(0, ly))] = hi
        ref[(*at, slice(None), slice(ly, 2 * ly))] = lo

    def wide(ref, f):
        return ref[f].reshape(rows, 2 * ly)

    def outer(f, v):
        return v[:, f * ly : (f + 1) * ly].reshape(lx, lz, ly)

    def flat(v):
        return v.reshape(rows, ly)

    def primitives(i, _=None):
        rho, e = mass[i], energy[i]
        m = [mt[k, i] for k in range(3)]
        inv = 1.0 / rho
        u = [a * inv for a in m]
        p = 0.4 * (e - 0.5 * (m[0] * u[0] + m[1] * u[1] + m[2] * u[2]))
        for k in range(3):
            xp[k, i + 3] = u[k]
            put(p2, (k, i), u[k])
        xp[3, i + 3] = p * inv
        put(p2, (3, i), p * inv)
        pt[i] = p
        ept[i] = e + p
        return 0

    for fetch in fetches:
        fetch.wait()
    edges = sorted({*range(3), *range(lx - 3, lx)})
    for i in edges:
        primitives(i)

    zeros3 = jnp.zeros((3, lz, ly), jnp.float32)

    def x_halo(ref, fields, base):
        to_next = pltpu.make_async_remote_copy(
            ref.at[:, pl.ds(lx, 3)], ref.at[:, pl.ds(0, 3)], hss.at[base], hrs.at[base],
            device_id={"gx": ix + 1}, device_id_type=MESH)
        to_prev = pltpu.make_async_remote_copy(
            ref.at[:, pl.ds(3, 3)], ref.at[:, pl.ds(lx + 3, 3)], hss.at[base + 1], hrs.at[base + 1],
            device_id={"gx": ix - 1}, device_id_type=MESH)

        @pl.when(ix == 0)
        def _():
            for f in range(fields):
                ref[f, 0:3] = zeros3

        @pl.when(ix == nx - 1)
        def _():
            for f in range(fields):
                ref[f, lx + 3 : lx + 6] = zeros3

        return to_next, to_prev, ix, nx

    def y_halo(source, ref, base):
        to_next = pltpu.make_async_remote_copy(
            source.at[pl.ds(16, 16)], ref.at[pl.ds(0, 16)], hss.at[base], hrs.at[base],
            device_id={"gy": iy + 1}, device_id_type=MESH)
        to_prev = pltpu.make_async_remote_copy(
            source.at[pl.ds(0, 16)], ref.at[pl.ds(16, 16)], hss.at[base + 1], hrs.at[base + 1],
            device_id={"gy": iy - 1}, device_id_type=MESH)

        @pl.when(iy == 0)
        def _():
            ref[0:16] = jnp.zeros((16, rows), jnp.float32)

        @pl.when(iy == ny - 1)
        def _():
            ref[16:32] = jnp.zeros((16, rows), jnp.float32)

        return to_next, to_prev, iy, ny

    def start(halo):
        to_next, to_prev, here, count = halo
        pl.when(here < count - 1)(to_next.start)
        pl.when(here > 0)(to_prev.start)

    def arrive(halo):
        to_next, to_prev, here, count = halo
        pl.when(here > 0)(to_next.wait_recv)
        pl.when(here < count - 1)(to_prev.wait_recv)

    def sent(halo):
        to_next, to_prev, here, count = halo
        pl.when(here < count - 1)(to_next.wait_send)
        pl.when(here > 0)(to_prev.wait_send)

    h1x = x_halo(xp, 4, 0)
    pl.semaphore_wait(barrier, nx + ny - 2)
    start(h1x)
    lax.fori_loop(3, lx - 3, primitives, 0, unroll=2)

    for fetch in small:
        fetch.wait()
    packed = dot(sel_tab[0], wide(p2, 0), NT)
    for f in range(1, 4):
        packed += dot(sel_tab[f], wide(p2, f), NT)
    ysend[...] = packed
    h1y = y_halo(ysend, yhalo, 2)
    start(h1y)
    for f in range(4):
        gy[f] = dot(wide(p2, f), dy_tab[...], NN).reshape(lx, lz, ly)
    arrive(h1y)
    rim = dot(jnp.concatenate(split(yhalo[...]), 0), ed_tab[:, : 4 * ly], TN)
    for f in range(4):
        gy[f] = (gy[f] + outer(f, rim)) * (1.0 / 60.0)
    arrive(h1x)

    def fluxes(i, _=None):
        u = [xp[k, i + 3] for k in range(3)]
        m = [mt[k, i] for k in range(3)]
        p, ep = pt[i], ept[i]
        g = [
            [difference(lambda k: xp[f, i + 3 + k]) for f in range(4)],
            [gy[f, i] for f in range(4)],
            [around(xp[f, i + 3]) for f in range(4)],
        ]
        dilation = (2.0 / 3.0 * viscosity) * (g[0][0] + g[1][1] + g[2][2])
        stress = {}
        for a in range(3):
            for b in range(a, 3):
                s = viscosity * (g[a][b] + g[b][a])
                if a == b:
                    s = s - dilation
                stress[a, b] = stress[b, a] = s
        for j in range(3):
            entries = [m[j]]
            for k in range(3):
                e = m[k] * u[j] - stress[k, j]
                entries.append(e + p if k == j else e)
            power = u[0] * stress[0, j] + u[1] * stress[1, j] + u[2] * stress[2, j]
            entries.append(ep * u[j] - power - conductivity * g[j][3])
            for c in range(5):
                if j == 0:
                    fxp[c, i + 3] = entries[c]
                elif j == 1:
                    put(f2, (c, i), entries[c])
                else:
                    dz[c, i] = around(entries[c])
        return 0

    for i in edges:
        fluxes(i)
    h2x = x_halo(fxp, 5, 4)
    start(h2x)
    lax.fori_loop(3, lx - 3, fluxes, 0)

    packed = dot(sel_tab[0], wide(f2, 0), NT)
    for f in range(1, 5):
        packed += dot(sel_tab[f], wide(f2, f), NT)
    ysend2[...] = packed
    h2y = y_halo(ysend2, yhalo2, 6)
    start(h2y)
    for c in range(5):
        dz[c] += dot(wide(f2, c), dy_tab[...], NN).reshape(lx, lz, ly) * (1.0 / 60.0)
    arrive(h2y)
    rim = dot(jnp.concatenate(split(yhalo2[...]), 0), ed_tab[...], TN)
    for c in range(5):
        dz[c] += outer(c, rim) * (1.0 / 60.0)
    arrive(h2x)

    width = 8 + 2 * (nx - 1)

    def xtab(k):
        return coef[ix * width + k]

    copies = []
    ends = {}
    for g, (f0, f1) in enumerate(GROUPS):
        v = [None] * 5
        for i in range(lx):
            for f in range(f0, f1):
                s = difference(lambda k: fxp[f, i + 3 + k]) + dz[f, i]
                s = s * (-2.0 * coefficient)
                v[f] = s if i == 0 else (s + coefficient * v[f]) * float(ipiv[i])
                inc[f, i] = v[f]
        last = list(v)
        for f in range(f0, f1):
            put(v2, (f, lx - 1), v[f])
        for i in range(lx - 2, -1, -1):
            for f in range(f0, f1):
                v[f] = inc[f, i] - float(coefficient * ipiv[i]) * v[f]
                put(v2, (f, i), v[f])
        for f in range(f0, f1):
            ends[f] = (v[f], last[f])
            xs[0, f] = xtab(0) * v[f] + xtab(1) * last[f]
            xs[1, f] = xtab(2) * v[f] + xtab(3) * last[f]
        for d in range(1, nx):
            which = jnp.where(ix + d >= nx, 1, 0).astype(jnp.int32)
            copy = pltpu.make_async_remote_copy(
                xs.at[which, pl.ds(f0, f1 - f0)], xr.at[d - 1, pl.ds(f0, f1 - f0)],
                xss.at[g, d - 1], xrs.at[g, d - 1],
                device_id={"gx": lax.rem(ix + d, nx)}, device_id_type=MESH)
            copy.start()
            copies.append((g, d, copy))

    edges_y = dot(wy_tab[0], wide(v2, 0), NT)
    for f in range(1, 5):
        edges_y += dot(wy_tab[f], wide(v2, f), NT)
    for f in range(5):
        both = dot(wide(v2, f), inv_tab[...], NN)
        inc[f] = (both[:, :ly] + both[:, ly:]).reshape(lx, lz, ly)
    outside_x = []
    edges_x = None
    for g, (f0, f1) in enumerate(GROUPS):
        for group, d, copy in copies:
            if group == g:
                copy.wait_recv()
        for f in range(f0, f1):
            y0, yl = ends[f]
            before = xtab(4) * y0 + xtab(5) * yl
            after = xtab(6) * y0 + xtab(7) * yl
            for d in range(1, nx):
                r = xr[d - 1, f]
                before += xtab(7 + d) * r
                after += xtab(7 + nx - 1 + d) * r
            pair = jnp.concatenate(split(jnp.concatenate([before, after], 0)), 1)
            outside_x.append(pair)
            part = dot(wy_tab[f], pair, NT)
            edges_x = part if edges_x is None else edges_x + part
    edges_x = edges_x[:16] + edges_x[16:]
    hi, lo = split(edges_x)
    edges_y = edges_y[:16] + edges_y[16:] + dot(jnp.concatenate([hi, lo, hi], 1), ex_tab[...], NN)

    ywidth = 8 + 2 * (ny - 1)

    def ytab(k):
        return coef[nx * width + iy * ywidth + k]

    y0, yl = edges_y[0:8], edges_y[8:16]
    ws[0] = ytab(0) * y0 + ytab(1) * yl
    ws[1] = ytab(2) * y0 + ytab(3) * yl
    ycopies = []
    for d in range(1, ny):
        which = jnp.where(iy + d >= ny, 1, 0).astype(jnp.int32)
        copy = pltpu.make_async_remote_copy(
            ws.at[which], wr.at[d - 1], wss.at[d - 1], wrs.at[d - 1],
            device_id={"gy": lax.rem(iy + d, ny)}, device_id_type=MESH)
        copy.start()
        ycopies.append(copy)
    both = dot(jnp.concatenate(outside_x, 0), inv_tab[...], NN)
    across = (both[:, :ly] + both[:, ly:]).reshape(5, 2, lz, ly)
    before = ytab(4) * y0 + ytab(5) * yl
    after = ytab(6) * y0 + ytab(7) * yl
    for d in range(1, ny):
        ycopies[d - 1].wait_recv()
        r = wr[d - 1]
        before += ytab(7 + d) * r
        after += ytab(7 + ny - 1 + d) * r
    hi, lo = split(jnp.concatenate([before, after], 0))
    rim = dot(jnp.concatenate([hi, lo, hi], 0), ey_tab[...], TN)
    stores = []
    for f in range(5):
        total = outer(f, rim)
        for i in range(lx):
            state = mass[i] if f == 0 else (energy[i] if f == 4 else mt[f - 1, i])
            step = float(xa[i]) * across[f, 0] + float(xb[i]) * across[f, 1]
            out[f, i] = (state + inc[f, i]) + (step + total[i])
        for z in range(lz):
            store = pltpu.make_async_copy(out.at[f, :, z, :], out_hbm.at[f, z], oss.at[f])
            store.start()
            stores.append(store)
    for store in stores:
        store.wait()

    for halo in (h1x, h1y, h2x, h2y):
        sent(halo)
    for _, _, copy in copies:
        copy.wait_send()
    for copy in ycopies:
        copy.wait_send()


def body(nx, ny, mass, mom, energy):
    lz, lx, ly = mass.shape
    rows = lx * lz
    coefficient = float(max(lx, ly))
    xtab, xa, xb = reduced_tables(lx, nx, coefficient)
    ytab, ya, yb = reduced_tables(ly, ny, coefficient)
    tables = lane_tables(lx, lz, ly, coefficient, xa, xb, ya, yb)
    coef = np.concatenate([xtab.reshape(-1), ytab.reshape(-1)])
    coef = np.pad(coef, (0, -coef.size % 1024))
    f32 = jnp.float32
    groups = len(GROUPS)
    block = (lx, lz, ly)
    dma = pltpu.SemaphoreType.DMA
    result = pl.pallas_call(
        functools.partial(kernel, nx, ny, lx, lz, ly, coefficient, pivots(lx, coefficient), xa, xb),
        out_shape=jax.ShapeDtypeStruct((5, lz, lx, ly), f32),
        in_specs=[pl.BlockSpec(memory_space=pltpu.HBM)] * 11,
        out_specs=pl.BlockSpec(memory_space=pltpu.HBM),
        scratch_shapes=[
            pltpu.VMEM(block, f32),
            pltpu.VMEM(block, f32),
            pltpu.SMEM(coef.shape, f32),
            *[pltpu.VMEM(t.shape, t.dtype) for t in tables],
            dma((9,)),
            dma((5,)),
            pltpu.VMEM((5, *block), f32),
            pltpu.VMEM((4, lx + 6, lz, ly), f32),
            pltpu.VMEM((4, lx, lz, 2 * ly), jnp.bfloat16),
            pltpu.VMEM(block, f32),
            pltpu.VMEM(block, f32),
            pltpu.VMEM((3, *block), f32),
            pltpu.VMEM((4, *block), f32),
            pltpu.VMEM((5, lx + 6, lz, ly), f32),
            pltpu.VMEM((5, lx, lz, 2 * ly), jnp.bfloat16),
            pltpu.VMEM((5, *block), f32),
            pltpu.VMEM((5, *block), f32),
            pltpu.VMEM((5, lx, lz, 2 * ly), jnp.bfloat16),
            pltpu.VMEM((32, rows), f32),
            pltpu.VMEM((32, rows), f32),
            pltpu.VMEM((32, rows), f32),
            pltpu.VMEM((32, rows), f32),
            pltpu.VMEM((2, 5, lz, ly), f32),
            pltpu.VMEM((nx - 1, 5, lz, ly), f32),
            pltpu.VMEM((2, 8, rows), f32),
            pltpu.VMEM((ny - 1, 8, rows), f32),
            dma((8,)),
            dma((8,)),
            dma((groups, nx - 1)),
            dma((groups, nx - 1)),
            dma((ny - 1,)),
            dma((ny - 1,)),
        ],
        compiler_params=pltpu.CompilerParams(
            collective_id=0, has_side_effects=True, vmem_limit_bytes=67043328
        ),
    )(
        mass, mom, energy,
        jnp.asarray(coef), *[jnp.asarray(t) for t in tables],
    )
    return result


def solution(mesh):
    return jax.shard_map(
        functools.partial(body, mesh.shape["gx"], mesh.shape["gy"]),
        mesh=mesh,
        in_specs=(P(None, "gx", "gy"), P(None, None, "gx", "gy"), P(None, "gx", "gy")),
        out_specs=P(None, None, "gx", "gy"),
        check_vma=False,
    )
```
